256 devices in a mesh: dp: 32 (over z_hi, x, core), tensor: 8 (over z_lo, y).
Axes of the slice: x: 4, y: 4, z: 8 (z_hi: 4, z_lo: 2; z = z_hi * 2 + z_lo), core: 2. Of those that a mesh axis runs over, the one named last changes fastest.
Arguments:
- quant_rows: int32 [32768, 2048], P(('dp', 'tensor')), may hold values from -127 to 127
- residual: bfloat16 [32768, 2048], P(('dp', 'tensor')), may hold values from -48 to 48
- row_scale: float32 [32768], P(('dp', 'tensor')), may hold values from 0.004 to 0.04
- norm_gain: float32 [2048], replicated, may hold values from 0.1 to 1.9
- gate_pre: bfloat16 [32768, 7168], P('dp', 'tensor'), may hold values from -6 to 6
- up_pre: bfloat16 [32768, 7168], P('dp', 'tensor'), may hold values from -6 to 6
- hidden_grad: bfloat16 [32768, 7168], P('dp', 'tensor'), may hold values from -6 to 6
- gate_weight: bfloat16 [2048, 7168], P('dp', 'tensor'), may hold values from -0.125 to 0.125
- up_weight: bfloat16 [2048, 7168], P('dp', 'tensor'), may hold values from -0.125 to 0.125
Outputs:
- resid_grad: bfloat16 [32768, 2048], P(('dp', 'tensor'))
- gate_weight_grad: float32 [2048, 7168], P('dp', 'tensor')
- up_weight_grad: float32 [2048, 7168], P('dp', 'tensor')
The draws below stay inside these ranges and needn't reach their ends.
All inputs are finite; a program needn't handle non-finite values.
Results may differ from the reference program's by a relative error of at most 0.014.
Values may be sent and summed in bfloat16 or wider, within the bound.
No kernel may reach another device: no remote copies, remote signals or barrier semaphores. Data moves between devices by JAX's collectives and lax.ppermute only.
A program may use at most 64 MiB of HBM per device.

```python
import math
import jax
import jax.numpy as jnp
from jax import lax

D = 2048
FF = 7168
TOK_DEV = 128
TOKENS = 32768
N_DP = 32
N_TENSOR = 8


def draw_residual(key, part):
    first_key, second_key, third_key = jax.random.split(jax.random.fold_in(key, 7), 3)
    row_scales = jnp.exp(jax.random.uniform(first_key, (TOKENS, 1), jnp.float32, math.log(0.3), math.log(3.0)))
    column_scales = jnp.exp(jax.random.uniform(second_key, (1, D), jnp.float32, math.log(0.3), math.log(3.0)))
    entries = jnp.clip(jax.random.normal(third_key, (TOKENS, D), jnp.float32), -4.0, 4.0)
    return (entries * row_scales * column_scales).astype(jnp.bfloat16)


def with_ends(result, rng, least, high):
    index_at = [jax.random.randint(jax.random.fold_in(rng, axis), (), 0, length) for axis, length in enumerate(result.shape)]
    widest = result.shape.index(max(result.shape))
    beside = index_at[:widest] + [(index_at[widest] + 1) % result.shape[widest]] + index_at[widest + 1:]
    return result.at[tuple(index_at)].set(least).at[tuple(beside)].set(high)


def shard_levels(key, shape, shards, least, top_value):
    def one(axis_at, parts):
        steps = jax.random.uniform(jax.random.fold_in(jax.random.fold_in(key, 6), axis_at), (parts,), jnp.float32, least / len(shards), top_value / len(shards))
        return jnp.repeat(jnp.exp(steps), shape[axis_at] // parts).reshape((-1,) + (1,) * (len(shape) - axis_at - 1))

    gain = one(*shards[0])
    for cut in shards[1:]:
        gain = gain * one(*cut)
    return gain


def centred(stream_key, shape, scale, reach, cuts=(), kind=jnp.bfloat16):
    result = scale * jax.random.normal(stream_key, shape, jnp.float32)
    if cuts:
        result = result * shard_levels(stream_key, shape, cuts, -0.22, 0.18)
    return jnp.clip(result, -reach, reach).astype(kind)


def setup_inputs(seed: int = 0) -> dict:
    seeds = jax.random.split(jax.random.key(seed), 10)
    quant_rows = with_ends(jax.random.randint(seeds[0], (TOKENS, D), -127, 128), jax.random.fold_in(seeds[0], 1), -127, 127).astype(jnp.int32)
    residual = draw_residual(jax.random.fold_in(seeds[9], 71), 0)
    row_scale = jnp.clip(jnp.exp(math.log(0.04) - 2.30258502 * jax.random.uniform(seeds[2], (TOKENS,), jnp.float32) ** shard_levels(seeds[2], (TOKENS,), ((0, 256),), -0.2, 0.2)), 0.004, 0.04)
    norm_gain = jnp.clip(1.0 + 0.18 * jax.random.normal(seeds[3], (D,), jnp.float32), 0.1, 1.9)
    gate_pre = centred(seeds[4], (TOKENS, FF), 1.0, 6.0, ((0, 32), (1, 8)))
    up_pre = centred(seeds[5], (TOKENS, FF), 1.0, 6.0, ((0, 32), (1, 8)))
    hidden_grad = centred(seeds[6], (TOKENS, FF), 1.0, 6.0, ((0, 32), (1, 8)))
    gate_weight = centred(seeds[7], (D, FF), D ** -0.5, 0.125, ((0, 32), (1, 8)))
    up_weight = centred(seeds[8], (D, FF), D ** -0.5, 0.125, ((0, 32), (1, 8)))
    return {"quant_rows": quant_rows, "residual": residual, "row_scale": row_scale, "norm_gain": norm_gain, "gate_pre": gate_pre, "up_pre": up_pre, "hidden_grad": hidden_grad, "gate_weight": gate_weight, "up_weight": up_weight}


def norm_rows(residual, quant_rows, row_scale, norm_gain):
    summed_in = residual.astype(jnp.float32) + quant_rows.astype(jnp.float32) * row_scale[:, None]
    inverse = lax.rsqrt(lax.optimization_barrier(jnp.mean(summed_in * summed_in, axis=-1, keepdims=True)) + 1e-05)
    unit_rows = summed_in * inverse
    return (unit_rows, inverse, (unit_rows * norm_gain).astype(jnp.bfloat16))

def reference(quant_rows, residual, row_scale, norm_gain, gate_pre, up_pre, hidden_grad, gate_weight, up_weight):
    slab_rows = TOK_DEV * N_TENSOR
    hidden_block = FF // N_TENSOR
    unit_rows, inverse, normed = norm_rows(residual, quant_rows, row_scale, norm_gain)

    def one_slab(carry_pair, slab_index):
        offset = (slab_index * slab_rows).astype(jnp.int32)

        def slab_part(array):
            return lax.dynamic_slice_in_dim(array, offset, slab_rows, 0)
        gate_val = slab_part(gate_pre).astype(jnp.float32)
        up_val = slab_part(up_pre).astype(jnp.float32)
        grad_val = slab_part(hidden_grad).astype(jnp.float32)
        sigmoid_gate = jax.nn.sigmoid(gate_val)
        up_grad = (grad_val * gate_val * sigmoid_gate).astype(jnp.bfloat16)
        gate_grad = (grad_val * up_val * sigmoid_gate * (1.0 + gate_val * (1.0 - sigmoid_gate))).astype(jnp.bfloat16)
        slab_normed = slab_part(normed)
        gate_part = jnp.dot(slab_normed.T, gate_grad, preferred_element_type=jnp.float32)
        up_part = jnp.dot(slab_normed.T, up_grad, preferred_element_type=jnp.float32)
        new_carry = (carry_pair[0] + lax.optimization_barrier(gate_part.astype(jnp.bfloat16)).astype(jnp.float32), carry_pair[1] + lax.optimization_barrier(up_part.astype(jnp.bfloat16)).astype(jnp.float32))
        normed_grad = jnp.zeros((slab_rows, D), jnp.float32)
        for shard_index in range(N_TENSOR):
            first_col = shard_index * hidden_block
            last_col = first_col + hidden_block
            partial_value = jnp.dot(gate_grad[:, first_col:last_col], gate_weight[:, first_col:last_col].T, preferred_element_type=jnp.float32)
            partial_value = partial_value + jnp.dot(up_grad[:, first_col:last_col], up_weight[:, first_col:last_col].T, preferred_element_type=jnp.float32)
            normed_grad = normed_grad + lax.optimization_barrier(partial_value.astype(jnp.bfloat16)).astype(jnp.float32)
        grad_term = norm_gain * normed_grad
        slab_unit = slab_part(unit_rows)
        slab_inverse = slab_part(inverse)
        input_grad = slab_inverse * (grad_term - slab_unit * lax.optimization_barrier(jnp.mean(slab_unit * grad_term, axis=-1, keepdims=True)))
        return (new_carry, input_grad.astype(jnp.bfloat16))
    zeros = jnp.zeros((D, FF), jnp.float32)
    totals, resid_grad = lax.scan(one_slab, (zeros, zeros), jnp.arange(N_DP, dtype=jnp.int32))
    factor = 1.0 / math.sqrt(TOKENS)
    return (resid_grad.reshape(TOKENS, D), totals[0] * factor, totals[1] * factor)
```

```python
import math

import jax
import jax.numpy as jnp
from jax import lax
from jax.experimental import pallas as pl
from jax.experimental.pallas import tpu as pltpu
from jax.sharding import PartitionSpec as P

NZ, NX, NC, NL, NY = 4, 4, 2, 2, 4
EPS = 1e-05


def dp_send(value, dz=0, dx=0, dc=0):
    pairs = []
    for z in range(NZ):
        for x in range(NX):
            for c in range(NC):
                to = (((z + dz) % NZ) * NX + (x + dx) % NX) * NC + (c + dc) % NC
                pairs.append(((z * NX + x) * NC + c, to))
    return lax.ppermute(value, "dp", pairs)


def tensor_send(value, dl=0, dy=0):
    pairs = []
    for l in range(NL):
        for y in range(NY):
            pairs.append((l * NY + y, ((l + dl) % NL) * NY + (y + dy) % NY))
    return lax.ppermute(value, "tensor", pairs)


def rows_of(ref):
    return ref[...].astype(jnp.float32)


def half_select(first, second):
    width = first.shape[1] // 2
    lane = lax.broadcasted_iota(jnp.int32, first.shape, 1)
    low = jnp.where(lane < width, first, pltpu.roll(second, width, 1))
    high = jnp.where(lane < width, pltpu.roll(first, width, 1), second)
    return low, high


def block_at(dp, dx, dz):
    z = lax.rem(dp // (NX * NC) + dz, NZ)
    x = lax.rem(lax.rem(dp // NC, NX) + dx, NX)
    return z * NX + x


def norm_kernel(dp_ref, quant_ref, resid_ref, scale_ref, gain_ref, out_ref, work):
    dp = dp_ref[0]
    core = lax.rem(dp, NC)
    blocks = NZ * NX
    wide = quant_ref.shape[1] // blocks
    half = quant_ref.shape[1] // 2
    summed = rows_of(resid_ref) + rows_of(quant_ref) * scale_ref[...]
    inverse = lax.rsqrt(jnp.mean(summed * summed, axis=-1, keepdims=True) + EPS)
    work[...] = summed * inverse * gain_ref[...]
    for k in range(blocks // 2):
        pair = []
        for j in (2 * k, 2 * k + 1):
            at = block_at(dp, j // NZ, j % NZ)
            pair.append(work[:, pl.ds(pl.multiple_of(at * wide, wide), wide)])
        low, high = half_select(*pair)
        mine = jnp.where(core == 0, low, high).astype(out_ref.dtype)
        other = jnp.where(core == 0, high, low).astype(out_ref.dtype)
        out_ref[:, k * wide : (k + 1) * wide] = mine
        out_ref[:, half + k * wide : half + (k + 1) * wide] = other


def grad_kernel(dp_ref, *refs):
    (quant_ref, resid_ref, scale_ref, gain_ref), keeps, came = refs[:4], refs[4:6], refs[6:8]
    out_ref, work = refs[8:]
    dp = dp_ref[0]
    core = lax.rem(dp, NC)
    blocks = NZ * NX
    wide = quant_ref.shape[1] // blocks
    for index, (keep_ref, came_ref) in enumerate(zip(keeps, came, strict=True)):
        for slot, dx in enumerate(PIECES[index]):
            for k in range(NZ // 2):
                base = slot * NZ * wide + k * wide
                got = []
                for side in range(2):
                    cols = slice(base + side * NZ // 2 * wide, base + side * NZ // 2 * wide + wide)
                    got.append(keep_ref[:, cols].astype(jnp.float32) + came_ref[:, cols].astype(jnp.float32))
                low = jnp.where(core == 0, got[0], got[1])
                high = jnp.where(core == 0, got[1], got[0])
                for j, block in enumerate(half_select(low, high)):
                    at = block_at(dp, dx, 2 * k + j)
                    work[:, pl.ds(pl.multiple_of(at * wide, wide), wide)] = block
    summed = rows_of(resid_ref) + rows_of(quant_ref) * scale_ref[...]
    inverse = lax.rsqrt(jnp.mean(summed * summed, axis=-1, keepdims=True) + EPS)
    unit = summed * inverse
    term = gain_ref[...] * work[...]
    result = inverse * (term - unit * jnp.mean(unit * term, axis=-1, keepdims=True))
    out_ref[...] = result.astype(out_ref.dtype)


PIECES = ((0, 1), (3, 2))


def row_calls(dp, quant_rows, residual, row_scale, norm_gain):
    rows, width = quant_rows.shape
    tile = rows // 2
    whole = lambda n: pl.BlockSpec((tile, n), lambda i, _: (i, 0))
    specs = [whole(width), whole(width), whole(1), pl.BlockSpec((1, width), lambda i, _: (0, 0))]
    args = (quant_rows, residual, row_scale.reshape(rows, 1), norm_gain.reshape(1, width))

    def call(kernel, extra):
        return pl.pallas_call(
            kernel,
            out_shape=jax.ShapeDtypeStruct((rows, width), jnp.bfloat16),
            grid_spec=pltpu.PrefetchScalarGridSpec(
                num_scalar_prefetch=1,
                grid=(rows // tile,),
                in_specs=specs + [whole(e.shape[1]) for e in extra],
                out_specs=whole(width),
                scratch_shapes=[pltpu.VMEM((tile, width), jnp.float32)],
            ),
            cost_estimate=pl.CostEstimate(
                flops=20 * rows * width, bytes_accessed=10 * rows * width, transcendentals=rows
            ),
        )(dp, *args, *extra)

    return call


def hidden_kernel(tensor_ref, gate_ref, up_ref, grad_ref, out_ref):
    width = gate_ref.shape[1]
    gate, up, grad = rows_of(gate_ref), rows_of(up_ref), rows_of(grad_ref)
    sig = jax.nn.sigmoid(gate)
    out_ref[:, :width] = (grad * up * sig * (1.0 + gate * (1.0 - sig))).astype(out_ref.dtype)
    out_ref[:, width:] = (grad * gate * sig).astype(out_ref.dtype)


def hidden_call(tensor, gate_pre, up_pre, hidden_grad):
    rows, width = gate_pre.shape
    tile = rows // (NL * NY)

    def source(i, tensor_ref):
        l = lax.rem(tensor_ref[0] // NY + lax.rem(i, NL), NL)
        y = lax.rem(lax.rem(tensor_ref[0], NY) + i // NL, NY)
        return (l * NY + y, 0)

    return pl.pallas_call(
        hidden_kernel,
        out_shape=jax.ShapeDtypeStruct((rows, 2 * width), jnp.bfloat16),
        grid_spec=pltpu.PrefetchScalarGridSpec(
            num_scalar_prefetch=1,
            grid=(NL * NY,),
            in_specs=[pl.BlockSpec((tile, width), source)] * 3,
            out_specs=pl.BlockSpec((tile, 2 * width), lambda i, _: (i, 0)),
        ),
        cost_estimate=pl.CostEstimate(
            flops=20 * rows * width, bytes_accessed=10 * rows * width, transcendentals=rows * width
        ),
    )(tensor, gate_pre, up_pre, hidden_grad)


def dot_t(a, b):
    return lax.dot_general(a, b, (((1,), (1,)), ((), ())), preferred_element_type=jnp.float32)


def dot_rows(a, b):
    return lax.dot_general(a, b, (((0,), (0,)), ((), ())), preferred_element_type=jnp.float32)


def cat(*parts, axis=0):
    return jnp.concatenate(parts, axis=axis)


def f32(v):
    return v.astype(jnp.float32)


def bf16(v):
    return v.astype(jnp.bfloat16)


def gather_weights(weight):
    rows = weight.shape[0]
    z1, z3, z2 = dp_send(weight, dz=-1), dp_send(weight, dz=1), dp_send(weight, dz=2)
    w0 = cat(weight, z1, z2, z3)
    w1, w3 = dp_send(w0, dx=-1), dp_send(w0, dx=1)
    w2 = cat(dp_send(w1[: 2 * rows], dx=-1), dp_send(w3[2 * rows :], dx=1))
    return {i: (w, dp_send(w, dc=1)) for i, w in ((0, w0), (1, w1), (3, w3), (2, w2))}


def gather_tokens(normed):
    rows = normed.shape[0]
    n0 = cat(normed, tensor_send(normed, dl=1))
    n1, n3 = tensor_send(n0, dy=-1), tensor_send(n0, dy=1)
    n2 = cat(tensor_send(n1[:rows], dy=-1), tensor_send(n3[rows:], dy=1))
    return cat(n0, n1, n2, n3)


def reduce_tokens(parts):
    rows = parts[0].shape[0] // (NL * NY)

    def block(first, count):
        return cat(*(p[first * rows : (first + count) * rows] for p in parts), axis=1)

    up, down = tensor_send(block(4, 1), dy=1), tensor_send(block(5, 1), dy=-1)
    ahead = cat(bf16(f32(block(2, 1)) + f32(up)), block(3, 1))
    back = cat(block(6, 1), bf16(f32(block(7, 1)) + f32(down)))
    from_down, from_up = tensor_send(ahead, dy=1), tensor_send(back, dy=-1)
    total = f32(block(0, 2)) + f32(from_down) + f32(from_up)
    return total[:rows], tensor_send(bf16(total[rows:]), dl=1)


def reduce_weights(normed, grad, factor):
    half = normed.shape[1] // 2
    block = half // NX
    away = dp_send(bf16(dot_rows(normed[:, half:], grad)), dc=1)

    def part(dx):
        at = slice(dx * block, (dx + 1) * block)
        return f32(bf16(dot_rows(normed[:, at], grad))) + f32(away[at])

    mid = block // 2
    far = bf16(part(2))
    up, down = dp_send(far[:mid], dx=1), dp_send(far[mid:], dx=-1)
    near, back = part(1), part(3)
    ahead = bf16(cat(near[:mid] + f32(up), near[mid:]))
    behind = bf16(cat(back[:mid], back[mid:] + f32(down)))
    from_down, from_up = dp_send(ahead, dx=1), dp_send(behind, dx=-1)
    total = part(0) + f32(from_down) + f32(from_up)
    rows = block // NZ
    got = [dp_send(bf16(total[k * rows : (k + 1) * rows]), dz=k) for k in (1, 3, 2)]
    return (total[:rows] + sum(f32(g) for g in got)) * factor


def body(
    quant_rows,
    residual,
    row_scale,
    norm_gain,
    gate_pre,
    up_pre,
    hidden_grad,
    gate_weight,
    up_weight,
):
    dp = lax.axis_index("dp").reshape(1)
    tensor = lax.axis_index("tensor").reshape(1)
    width = gate_pre.shape[1]
    factor = 1.0 / math.sqrt(gate_pre.shape[0] * lax.axis_size("dp"))
    row_call = row_calls(dp, quant_rows, residual, row_scale, norm_gain)

    weights = gather_weights(cat(gate_weight, up_weight, axis=1))
    normed = gather_tokens(row_call(norm_kernel, ()))
    grads = hidden_call(tensor, gate_pre, up_pre, hidden_grad)

    kept, came = [], []
    for piece in PIECES:
        parts = [bf16(dot_t(grads, w)) for dx in piece for w in weights[dx]]
        own, other = reduce_tokens(parts)
        kept.append(own)
        came.append(other)
    resid_grad = row_call(grad_kernel, (*kept, *came))
    gate_out = reduce_weights(normed, grads[:, :width], factor)
    up_out = reduce_weights(normed, grads[:, width:], factor)
    return resid_grad, gate_out, up_out


def solution(mesh):
    rows, block = P(("dp", "tensor"), None), P("dp", "tensor")
    return jax.shard_map(
        body,
        mesh=mesh,
        in_specs=(rows, rows, P(("dp", "tensor")), P(), block, block, block, block, block),
        out_specs=(rows, block, block),
        check_vma=False,
    )
```

```python
import math

import jax
import jax.numpy as jnp
from jax import lax
from jax.experimental import pallas as pl
from jax.experimental.pallas import tpu as pltpu
from jax.experimental.layout import Layout, with_layout_constraint
from jax.sharding import PartitionSpec as P


NZ, NX, NC, NL, NY = 4, 4, 2, 2, 4
EPS = 1e-05

Y_GROUPS = [[l * NY + y for y in range(NY)] for l in range(NL)]
PIECES = (0, 1, 3, 2)


def dp_send(value, dz=0, dx=0, dc=0):
    pairs = []
    for z in range(NZ):
        for x in range(NX):
            for c in range(NC):
                to = (((z + dz) % NZ) * NX + (x + dx) % NX) * NC + (c + dc) % NC
                pairs.append(((z * NX + x) * NC + c, to))
    return lax.ppermute(value, "dp", pairs)


def layer_swap(value):
    return lax.ppermute(value, "tensor", [(i, (i + NY) % (NL * NY)) for i in range(NL * NY)])


def exchange(value):
    return lax.all_to_all(value, "tensor", 0, 0, axis_index_groups=Y_GROUPS, tiled=True)


def rows_major(value):
    return with_layout_constraint(value, Layout(major_to_minor=tuple(range(value.ndim))))


def after(value, *earlier):
    return lax.optimization_barrier((value, earlier))[0]


def f32(v):
    return v.astype(jnp.float32)


def bf16(v):
    return v.astype(jnp.bfloat16)


def cat(*parts, axis=0):
    return jnp.concatenate(parts, axis=axis)


def half_select(first, second):
    width = first.shape[1] // 2
    lane = lax.broadcasted_iota(jnp.int32, first.shape, 1)
    low = jnp.where(lane < width, first, pltpu.roll(second, width, 1))
    high = jnp.where(lane < width, pltpu.roll(first, width, 1), second)
    return low, high


def block_at(dp, dx, dz, wide):
    z = lax.rem(dp // (NX * NC) + dz, NZ)
    x = lax.rem(lax.rem(dp // NC, NX) + dx, NX)
    return pl.ds(pl.multiple_of((z * NX + x) * wide, wide), wide)


def unit_rows(quant_ref, resid_ref, scale_ref):
    summed = f32(resid_ref[...]) + f32(quant_ref[...]) * scale_ref[...]
    inverse = lax.rsqrt(jnp.mean(summed * summed, axis=-1, keepdims=True) + EPS)
    return summed * inverse, inverse


def norm_kernel(dp_ref, quant_ref, resid_ref, scale_ref, gain_ref, mine_ref, other_ref, work):
    dp = dp_ref[0]
    first = lax.rem(dp, NC) == 0
    wide = quant_ref.shape[1] // (NZ * NX)
    unit, _ = unit_rows(quant_ref, resid_ref, scale_ref)
    work[...] = unit * gain_ref[...]
    for k in range(NZ * NX // 2):
        pair = (work[:, block_at(dp, j // NZ, j % NZ, wide)] for j in (2 * k, 2 * k + 1))
        low, high = half_select(*pair)
        at = slice(k * wide, (k + 1) * wide)
        mine_ref[:, at] = bf16(jnp.where(first, low, high))
        other_ref[:, at] = bf16(jnp.where(first, high, low))


def grad_kernel(dp_ref, quant_ref, resid_ref, scale_ref, gain_ref, kept_ref, layer_ref, core_ref, out_ref, work):
    dp = dp_ref[0]
    first = lax.rem(dp, NC) == 0
    wide = quant_ref.shape[1] // (NZ * NX)
    for k in range(NZ * NX // 2):
        at = slice(k * wide, (k + 1) * wide)
        own, came = kept_ref[:, at] + f32(layer_ref[:, at]), f32(core_ref[:, at])
        pair = half_select(jnp.where(first, own, came), jnp.where(first, came, own))
        for j, block in zip((2 * k, 2 * k + 1), pair, strict=True):
            work[:, block_at(dp, PIECES[j // NZ], j % NZ, wide)] = block
    unit, inverse = unit_rows(quant_ref, resid_ref, scale_ref)
    term = gain_ref[...] * work[...]
    out_ref[...] = bf16(inverse * (term - unit * jnp.mean(unit * term, axis=-1, keepdims=True)))


def row_calls(dp, quant_rows, residual, row_scale, norm_gain):
    rows, width = quant_rows.shape
    tile = 16
    whole = lambda n: pl.BlockSpec((tile, n), lambda i, _: (i, 0))
    specs = [whole(width), whole(width), whole(1), pl.BlockSpec((1, width), lambda i, _: (0, 0))]
    args = (quant_rows, residual, row_scale.reshape(rows, 1), norm_gain.reshape(1, width))

    def call(kernel, extra, widths):
        return pl.pallas_call(
            kernel,
            out_shape=[jax.ShapeDtypeStruct((rows, n), jnp.bfloat16) for n in widths],
            grid_spec=pltpu.PrefetchScalarGridSpec(
                num_scalar_prefetch=1,
                grid=(rows // tile,),
                in_specs=specs + [whole(e.shape[1]) for e in extra],
                out_specs=[whole(n) for n in widths],
                scratch_shapes=[pltpu.VMEM((tile, width), jnp.float32)],
            ),
            cost_estimate=pl.CostEstimate(
                flops=20 * rows * width, bytes_accessed=10 * rows * width, transcendentals=rows
            ),
        )(dp, *args, *extra)

    return call


def hidden_kernel(gate_ref, up_ref, grad_ref, out_ref):
    width = gate_ref.shape[1]
    gate, up, grad = f32(gate_ref[...]), f32(up_ref[...]), f32(grad_ref[...])
    sig = 0.5 * jnp.tanh(0.5 * gate) + 0.5
    scaled = grad * sig
    out_ref[:, :width] = bf16(scaled * up * (1.0 + gate * (1.0 - sig)))
    out_ref[:, width:] = bf16(scaled * gate)


def hidden_call(gate_pre, up_pre, hidden_grad):
    rows, width = gate_pre.shape
    tile = rows // (NL * NY)
    return pl.pallas_call(
        hidden_kernel,
        out_shape=jax.ShapeDtypeStruct((rows, 2 * width), jnp.bfloat16),
        grid=(NL * NY,),
        in_specs=[pl.BlockSpec((tile, width), lambda i: (lax.rem(i, NL) * NY + i // NL, 0))] * 3,
        out_specs=pl.BlockSpec((tile, 2 * width), lambda i: (i, 0)),
        cost_estimate=pl.CostEstimate(
            flops=20 * rows * width, bytes_accessed=10 * rows * width, transcendentals=rows * width
        ),
    )(gate_pre, up_pre, hidden_grad)


def dot_t(a, b):
    return lax.dot_general(a, b, (((1,), (1,)), ((), ())), preferred_element_type=jnp.float32)


def dot_rows(a, b):
    return lax.dot_general(a, b, (((0,), (0,)), ((), ())), preferred_element_type=jnp.float32)


def gather_weights(weight):
    rows = weight.shape[0]
    z1, z3, z2 = dp_send(weight, dz=-1), dp_send(weight, dz=1), dp_send(weight, dz=2)
    w0 = cat(weight, z1, z2, z3)
    w1, w3 = dp_send(w0, dx=-1), dp_send(w0, dx=1)
    w2 = cat(dp_send(w1[: 2 * rows], dx=-1), dp_send(w3[2 * rows :], dx=1))
    return cat(w0, w1, w3, w2)


def gather_tokens(block, layer, *earlier):
    rows, width = block.shape
    came = layer_swap(block)
    pair = cat(jnp.where(layer == 0, block, came), jnp.where(layer == 0, came, block))
    spread = after(jnp.broadcast_to(pair, (NY, *pair.shape)), *earlier)
    return exchange(spread).reshape(NY * NL * rows, width)


def reduce_tokens(part, layer, earlier):
    rows, width = part.shape
    by_y = rows_major(exchange(after(rows_major(part).reshape(NY, rows // NY, width), earlier)))
    size = rows // (NY * NL)

    def total(which):
        return f32(lax.dynamic_slice_in_dim(by_y, which * size, size, 1)).sum(0)

    return total(layer), layer_swap(bf16(total(1 - layer))), by_y


def reduce_weights(part, factor):
    block = part.shape[0] // NX
    mid = block // 2

    def at(dx, first=0, last=block):
        return part[dx * block + first : dx * block + last]

    up, down = dp_send(at(2, 0, mid), dx=1), dp_send(at(2, mid), dx=-1)
    ahead = cat(bf16(f32(at(1, 0, mid)) + f32(up)), at(1, mid))
    behind = cat(at(3, 0, mid), bf16(f32(at(3, mid)) + f32(down)))
    from_down, from_up = dp_send(ahead, dx=1), dp_send(behind, dx=-1)
    total = f32(at(0)) + f32(from_down) + f32(from_up)
    rows = block // NZ
    got = [dp_send(bf16(total[k * rows : (k + 1) * rows]), dz=k) for k in (1, 3, 2)]
    return (total[:rows] + sum(f32(g) for g in got)) * factor


def body(
    quant_rows,
    residual,
    row_scale,
    norm_gain,
    gate_pre,
    up_pre,
    hidden_grad,
    gate_weight,
    up_weight,
):
    dp = lax.axis_index("dp").reshape(1)
    layer = lax.div(lax.axis_index("tensor"), NY)
    model_width = quant_rows.shape[1]
    half = model_width // NC
    width = gate_pre.shape[1]
    factor = 1.0 / math.sqrt(gate_pre.shape[0] * lax.axis_size("dp"))
    row_call = row_calls(dp, quant_rows, residual, row_scale, norm_gain)

    mine, other = row_call(norm_kernel, (), (half, half))
    theirs = dp_send(other, dc=1)
    weights = gather_weights(cat(gate_weight, up_weight, axis=1))
    grads = hidden_call(after(gate_pre, other), up_pre, hidden_grad)
    their_grads = dp_send(grads, dc=1)
    first = gather_tokens(mine, layer)
    normed = first, gather_tokens(theirs, layer, first)

    def weight_part(at):
        first = bf16(dot_rows(normed[0], grads[:, at]))
        return reduce_weights(bf16(dot_rows(normed[1], their_grads[:, at]) + f32(first)), factor)

    kept, came, moved = reduce_tokens(bf16(dot_t(their_grads, weights)), layer, normed[1])
    across = dp_send(bf16(kept + f32(came)), dc=1)
    own = reduce_tokens(bf16(dot_t(grads, weights)), layer, moved)[:2]
    gate_out, up_out = weight_part(slice(width)), weight_part(slice(width, None))
    (resid_grad,) = row_call(grad_kernel, (*own, across), (model_width,))
    return resid_grad, gate_out, up_out


def solution(mesh):
    rows, block = P(("dp", "tensor"), None), P("dp", "tensor")

    return jax.shard_map(
        body,
        mesh=mesh,
        in_specs=(rows, rows, P(("dp", "tensor")), P(), block, block, block, block, block),
        out_specs=(rows, block, block),
        check_vma=False,
    )
```

```python
import math

import jax
import jax.numpy as jnp
from jax import lax
from jax.experimental import pallas as pl
from jax.experimental.pallas import tpu as pltpu
from jax.experimental.layout import Layout, with_layout_constraint
from jax.sharding import PartitionSpec as P


NZ, NX, NC, NL, NY = 4, 4, 2, 2, 4
EPS = 1e-05

PIECES = (0, 1, 3, 2)


def dp_send(value, dz=0, dx=0, dc=0):
    pairs = []
    for z in range(NZ):
        for x in range(NX):
            for c in range(NC):
                to = (((z + dz) % NZ) * NX + (x + dx) % NX) * NC + (c + dc) % NC
                pairs.append(((z * NX + x) * NC + c, to))
    return lax.ppermute(value, "dp", pairs)


def tensor_send(value, dl=0, dy=0):
    pairs = []
    for l in range(NL):
        for y in range(NY):
            pairs.append((l * NY + y, ((l + dl) % NL) * NY + (y + dy) % NY))
    return lax.ppermute(value, "tensor", pairs)


def rows_major(value):
    return with_layout_constraint(value, Layout(major_to_minor=tuple(range(value.ndim))))


def after(value, *earlier):
    return lax.optimization_barrier((value, earlier))[0]


def f32(v):
    return v.astype(jnp.float32)


def bf16(v):
    return v.astype(jnp.bfloat16)


def cat(*parts, axis=0):
    return jnp.concatenate(parts, axis=axis)


def half_select(first, second):
    width = first.shape[1] // 2
    lane = lax.broadcasted_iota(jnp.int32, first.shape, 1)
    low = jnp.where(lane < width, first, pltpu.roll(second, width, 1))
    high = jnp.where(lane < width, pltpu.roll(first, width, 1), second)
    return low, high


def block_at(dp, dx, dz, wide):
    z = lax.rem(dp // (NX * NC) + dz, NZ)
    x = lax.rem(lax.rem(dp // NC, NX) + dx, NX)
    return pl.ds(pl.multiple_of((z * NX + x) * wide, wide), wide)


CHUNK = 16


def unit_rows(at, quant_ref, resid_ref, scale_ref):
    scale = scale_ref[0]
    row = at + lax.broadcasted_iota(jnp.int32, (CHUNK, scale.shape[1]), 0)
    lane = lax.broadcasted_iota(jnp.int32, (CHUNK, scale.shape[1]), 1)
    column = jnp.sum(jnp.where(row == lane, scale, 0.0), axis=1, keepdims=True)
    rows = pl.ds(at, CHUNK)
    summed = f32(resid_ref[rows, :]) + f32(quant_ref[rows, :]) * column
    inverse = lax.rsqrt(jnp.mean(summed * summed, axis=-1, keepdims=True) + EPS)
    return summed * inverse, inverse


def chunks(ref, step):
    def run(i, carry):
        step(pl.multiple_of(i * CHUNK, CHUNK))
        return carry

    lax.fori_loop(0, ref.shape[0] // CHUNK, run, 0)


def norm_kernel(dp_ref, quant_ref, resid_ref, scale_ref, gain_ref, gate_ref, up_ref, mine_ref, other_ref, weight_ref, work):
    dp = dp_ref[0]
    first = lax.rem(dp, NC) == 0
    wide = quant_ref.shape[1] // (NZ * NX)
    weight_ref[:, : gate_ref.shape[1]] = gate_ref[...]
    weight_ref[:, gate_ref.shape[1] :] = up_ref[...]

    def step(at):
        unit, _ = unit_rows(at, quant_ref, resid_ref, scale_ref)
        work[...] = unit * gain_ref[...]
        for k in range(NZ * NX // 2):
            pair = (work[:, block_at(dp, j // NZ, j % NZ, wide)] for j in (2 * k, 2 * k + 1))
            low, high = half_select(*pair)
            to = pl.ds(at, CHUNK), slice(k * wide, (k + 1) * wide)
            mine_ref[to] = bf16(jnp.where(first, low, high))
            other_ref[to] = bf16(jnp.where(first, high, low))

    chunks(quant_ref, step)


def grad_kernel(dp_ref, quant_ref, resid_ref, scale_ref, gain_ref, kept_ref, layer_ref, core_ref, out_ref, work):
    dp = dp_ref[0]
    first = lax.rem(dp, NC) == 0
    wide = quant_ref.shape[1] // (NZ * NX)

    def step(at):
        rows = pl.ds(at, CHUNK)
        for k in range(NZ * NX // 2):
            part = rows, slice(k * wide, (k + 1) * wide)
            own, came = kept_ref[part] + f32(layer_ref[part]), f32(core_ref[part])
            pair = half_select(jnp.where(first, own, came), jnp.where(first, came, own))
            for j, block in zip((2 * k, 2 * k + 1), pair, strict=True):
                work[:, block_at(dp, PIECES[j // NZ], j % NZ, wide)] = block
        unit, inverse = unit_rows(at, quant_ref, resid_ref, scale_ref)
        term = gain_ref[...] * work[...]
        mean = jnp.mean(unit * term, axis=-1, keepdims=True)
        out_ref[rows, :] = bf16(inverse * (term - unit * mean))

    chunks(quant_ref, step)


def row_calls(dp, quant_rows, residual, row_scale, norm_gain):
    rows, width = quant_rows.shape
    steps = 2
    tile = rows // steps
    whole = lambda n, m: pl.BlockSpec((m // steps, n), lambda i, _: (i, 0))
    specs = [
        whole(width, rows),
        whole(width, rows),
        pl.BlockSpec((1, 1, tile), lambda i, _: (i, 0, 0)),
        pl.BlockSpec((1, width), lambda i, _: (0, 0)),
    ]
    args = (quant_rows, residual, row_scale.reshape(steps, 1, tile), norm_gain.reshape(1, width))

    def call(kernel, extra, outs):
        return pl.pallas_call(
            kernel,
            out_shape=[jax.ShapeDtypeStruct(o, jnp.bfloat16) for o in outs],
            grid_spec=pltpu.PrefetchScalarGridSpec(
                num_scalar_prefetch=1,
                grid=(steps,),
                in_specs=specs + [whole(e.shape[1], e.shape[0]) for e in extra],
                out_specs=[whole(n, m) for m, n in outs],
                scratch_shapes=[pltpu.VMEM((CHUNK, width), jnp.float32)],
            ),
            cost_estimate=pl.CostEstimate(
                flops=20 * rows * width, bytes_accessed=10 * rows * width, transcendentals=rows
            ),
        )(dp, *args, *extra)

    return call


def hidden_kernel(tensor_ref, gate_ref, up_ref, grad_ref, out_ref):
    width = gate_ref.shape[1]
    gate, up, grad = f32(gate_ref[...]), f32(up_ref[...]), f32(grad_ref[...])
    sig = 0.5 * jnp.tanh(0.5 * gate) + 0.5
    scaled = grad * sig
    out_ref[:, :width] = bf16(scaled * up * (1.0 + gate * (1.0 - sig)))
    out_ref[:, width:] = bf16(scaled * gate)


def hidden_call(tensor, gate_pre, up_pre, hidden_grad):
    rows, width = gate_pre.shape
    tile = rows // (NL * NY)

    def source(i, tensor_ref):
        l = lax.rem(lax.div(tensor_ref[0], NY) + lax.rem(i, NL), NL)
        y = lax.rem(lax.rem(tensor_ref[0], NY) + lax.div(i, NL), NY)
        return (l * NY + y, 0)

    return pl.pallas_call(
        hidden_kernel,
        out_shape=jax.ShapeDtypeStruct((rows, 2 * width), jnp.bfloat16),
        grid_spec=pltpu.PrefetchScalarGridSpec(
            num_scalar_prefetch=1,
            grid=(NL * NY,),
            in_specs=[pl.BlockSpec((tile, width), source)] * 3,
            out_specs=pl.BlockSpec((tile, 2 * width), lambda i, _: (i, 0)),
        ),
        cost_estimate=pl.CostEstimate(
            flops=20 * rows * width, bytes_accessed=10 * rows * width, transcendentals=rows * width
        ),
    )(tensor, gate_pre, up_pre, hidden_grad)


def dot_t(a, b):
    return lax.dot_general(a, b, (((1,), (1,)), ((), ())), preferred_element_type=jnp.float32)


def dot_rows(a, b):
    return lax.dot_general(a, b, (((0,), (0,)), ((), ())), preferred_element_type=jnp.float32)


def weight_kernel(normed_ref, their_normed_ref, grad_ref, their_grad_ref, out_ref):
    out_ref[...] = bf16(
        dot_rows(normed_ref[...], grad_ref[...]) + dot_rows(their_normed_ref[...], their_grad_ref[...])
    )


def weight_call(normed, grads, column):
    tokens, rows = normed[0].shape
    width = grads[0].shape[1] // 2
    tile = rows // 4
    return pl.pallas_call(
        weight_kernel,
        out_shape=jax.ShapeDtypeStruct((rows, width), jnp.bfloat16),
        grid=(rows // tile,),
        in_specs=[pl.BlockSpec((tokens, tile), lambda i: (0, i))] * 2
        + [pl.BlockSpec((tokens, width), lambda i: (0, column))] * 2,
        out_specs=pl.BlockSpec((tile, width), lambda i: (i, 0)),
        cost_estimate=pl.CostEstimate(
            flops=4 * tokens * rows * width,
            bytes_accessed=2 * (2 * tokens + width) * rows + 8 * tokens * width,
            transcendentals=0,
        ),
    )(*normed, *grads)


def gather_weights(weight):
    rows = weight.shape[0]
    z1, z3, z2 = dp_send(weight, dz=-1), dp_send(weight, dz=1), dp_send(weight, dz=2)
    w0 = cat(weight, z1, z2, z3)
    w1, w3 = dp_send(w0, dx=-1), dp_send(w0, dx=1)
    w2 = cat(dp_send(w1[: 2 * rows], dx=-1), dp_send(w3[2 * rows :], dx=1))
    return cat(w0, w1, w3, w2)


def gather_tokens(mine, theirs):
    rows = mine.shape[0]
    came = tensor_send(cat(mine, theirs), dl=1)
    n0 = cat(mine, came[:rows], theirs, came[rows:])
    half = 2 * rows
    n1, n3 = tensor_send(n0, dy=-1), tensor_send(n0, dy=1)
    far = tensor_send(n1[:half], dy=-1), tensor_send(n3[half:], dy=1)
    return tuple(
        cat(n0[at], n1[at], middle, n3[at])
        for at, middle in zip((slice(half), slice(half, None)), far, strict=True)
    )


def reduce_tokens(theirs, own):
    rows = own.shape[0] // NY
    at = lambda part, dy: part[dy * rows : (dy + 1) * rows]
    t_far, t_back = tensor_send(at(theirs, 2), dy=1), tensor_send(at(theirs, 3), dy=-1)
    o_far, o_ahead = tensor_send(at(own, 2), dy=-1), tensor_send(at(own, 1), dy=1)
    t_ahead = tensor_send(bf16(f32(at(theirs, 1)) + f32(t_far)), dy=1)
    o_back = tensor_send(bf16(f32(at(own, 3)) + f32(o_far)), dy=-1)
    results = []
    for part, *got in ((theirs, t_back, t_ahead), (own, o_ahead, o_back)):
        total = lambda where: sum(f32(v[where]) for v in (at(part, 0), *got))
        came = tensor_send(bf16(total(slice(rows // NL, None))), dl=1)
        results.append((total(slice(rows // NL)), came))
    return results


def reduce_weights(part, factor):
    block = part.shape[0] // NX
    mid = block // 2

    def at(dx, first=0, last=block):
        return part[dx * block + first : dx * block + last]

    up, down = dp_send(at(2, 0, mid), dx=1), dp_send(at(2, mid), dx=-1)
    ahead = cat(bf16(f32(at(1, 0, mid)) + f32(up)), at(1, mid))
    behind = cat(at(3, 0, mid), bf16(f32(at(3, mid)) + f32(down)))
    from_down, from_up = dp_send(ahead, dx=1), dp_send(behind, dx=-1)
    total = f32(at(0)) + f32(from_down) + f32(from_up)
    rows = block // NZ
    got = [dp_send(bf16(total[k * rows : (k + 1) * rows]), dz=k) for k in (1, 3, 2)]
    return (total[:rows] + sum(f32(g) for g in got)) * factor


def body(
    quant_rows,
    residual,
    row_scale,
    norm_gain,
    gate_pre,
    up_pre,
    hidden_grad,
    gate_weight,
    up_weight,
):
    dp = lax.axis_index("dp").reshape(1)
    tensor = lax.axis_index("tensor").reshape(1)
    rows, model_width = quant_rows.shape
    width = gate_pre.shape[1]
    factor = 1.0 / math.sqrt(gate_pre.shape[0] * lax.axis_size("dp"))
    row_call = row_calls(dp, quant_rows, residual, row_scale, norm_gain)

    block = (rows, model_width // NC)
    mine, other, weight = row_call(
        norm_kernel, (gate_weight, up_weight), (block, block, (gate_weight.shape[0], 2 * width))
    )
    theirs = dp_send(other, dc=1)
    weights = gather_weights(weight)
    grads = hidden_call(tensor, after(gate_pre, other), up_pre, hidden_grad)
    their_grads = dp_send(grads, dc=1)
    normed = gather_tokens(mine, theirs)

    their_part = rows_major(bf16(dot_t(their_grads, weights)))
    own_part = rows_major(bf16(dot_t(grads, weights)))
    (kept, came), own = reduce_tokens(their_part, own_part)
    across = dp_send(bf16(kept + f32(came)), dc=1)
    outs = []
    for h in range(2):
        part = weight_call(normed, (grads, their_grads), h)
        outs.append(reduce_weights(part, factor))
    (resid_grad,) = row_call(grad_kernel, (*own, across), ((rows, model_width),))
    return resid_grad, *outs


def solution(mesh):
    rows, block = P(("dp", "tensor"), None), P("dp", "tensor")

    return jax.shard_map(
        body,
        mesh=mesh,
        in_specs=(rows, rows, P(("dp", "tensor")), P(), block, block, block, block, block),
        out_specs=(rows, block, block),
        check_vma=False,
    )
```
